512 devices in a mesh: dom: 512 (over x, y, z, core).
Axes of the slice: x: 4, y: 8, z: 8, core: 2. Of those that a mesh axis runs over, the one named last changes fastest.
Arguments:
- features: bfloat16 [589824, 128], P('dom'), may hold values from -6 to 6
- targets: bfloat16 [589824, 128], P('dom'), may hold values from -6 to 6
- first_weight: bfloat16 [128, 128], replicated, may hold values from -0.5 to 0.5
- second_weight: bfloat16 [128, 128], replicated, may hold values from -0.5 to 0.5
- local_bonds: bfloat16 [589824, 1152], P('dom'), may hold values from -0.4375 to 0.4375
- halo_bonds: bfloat16 [589824, 512], P('dom'), may hold values from -0.4375 to 0.4375
- tile_mask: int32 [9216, 18], P('dom'), may hold values 0 or 1
- send_rows: int32 [2048, 128], P('dom'), may hold values from 0 to 1151
Outputs:
- prediction: bfloat16 [589824, 128], P('dom')
- grad_first: float32 [128, 128], replicated
- grad_second: float32 [128, 128], replicated
The draws below stay inside these ranges and needn't reach their ends.
Inputs may be any that keep to these rules, and one draw needn't show every extreme that they name: `tile_mask`: tile presence flags. `send_rows`: local atom numbers of the sending partition; repeats allowed.
All inputs are finite; a program needn't handle non-finite values. No bound on the sum of `tile_mask` on one device may be relied on, other than what follows from the above.
Results may differ from the reference program's by a relative error of at most 0.004.
The reference program's roundings to bfloat16 on the way count: a program that leaves them out, or rounds other values in their place, can miss the bound.
Values may be sent and summed in bfloat16 or wider, within the bound.
A program may use at most 64 MiB of HBM per device.

```python
import math
import jax
import jax.numpy as jnp
from jax import lax

H = 128
NODE_DEV = 1152
HALO = 128
ROUNDS = 4
TILES_DEV = 18
NODES = 589824
N_DOM = 512


def with_ends(entries, key, low, top_value):
    longest = entries.shape.index(max(entries.shape))
    spots = []
    for shift in (0, 1):
        where = [jax.random.randint(jax.random.fold_in(key, axis), (), 0, length) for axis, length in enumerate(entries.shape)]
        where[longest] = (where[longest] + shift) % entries.shape[longest]
        spots.append(tuple(where))
    return entries.at[spots[0]].set(low).at[spots[1]].set(top_value)


def block_levels(key, shape, split, smallest, high):
    loudness, own = 1.0, jax.random.fold_in(key, 6)
    for dim, parts in split:
        heights = jnp.exp(jax.random.uniform(jax.random.fold_in(own, dim), (parts,), jnp.float32, smallest / len(split), high / len(split)))
        loudness = loudness * jnp.repeat(heights, shape[dim] // parts).reshape([-1 if axis == dim else 1 for axis in range(len(shape))])
    return loudness


def scatter_about(own_key, extent, spread, most, cuts=(), kind=jnp.bfloat16):
    loudness = block_levels(own_key, extent, cuts, -0.22, 0.18) if cuts else 1.0
    result = jax.random.normal(own_key, extent, jnp.float32) * spread * loudness
    return jnp.minimum(jnp.maximum(result, -most), most).astype(kind)


def setup_inputs(seed: int = 0) -> dict:
    key_list = jax.random.split(jax.random.key(seed), 9)
    return {
        "features": scatter_about(key_list[0], (NODES, H), 1.0, 6.0, ((0, 512),)),
        "targets": scatter_about(key_list[1], (NODES, H), 1.0, 6.0, ((0, 512),)),
        "first_weight": scatter_about(key_list[2], (H, H), H ** -0.5, 0.5),
        "second_weight": scatter_about(key_list[3], (H, H), H ** -0.5, 0.5),
        "local_bonds": scatter_about(key_list[4], (NODES, NODE_DEV), ((NODE_DEV // 2 + ROUNDS * HALO) ** -0.5), 0.4375, ((0, 512),)),
        "halo_bonds": scatter_about(key_list[5], (NODES, ROUNDS * HALO), ((NODE_DEV // 2 + ROUNDS * HALO) ** -0.5), 0.4375, ((0, 512),)),
        "tile_mask": with_ends((jax.random.randint(key_list[6], (N_DOM * TILES_DEV, TILES_DEV), 0, 2) < 1).astype(jnp.int32), jax.random.fold_in(key_list[6], 1), 0, 1),
        "send_rows": with_ends(jax.random.randint(key_list[7], (N_DOM * ROUNDS, HALO), 0, NODE_DEV), jax.random.fold_in(key_list[7], 1), 0, NODE_DEV - 1).astype(jnp.int32),
    }


def expand_mask(mask):
    return jnp.repeat(jnp.repeat(mask, 64, axis=0), 64, axis=1).astype(jnp.bfloat16)

def reference(features, targets, first_weight, second_weight, local_bonds, halo_bonds, tile_mask, send_rows):
    bond_all = local_bonds.reshape(N_DOM, NODE_DEV, NODE_DEV)
    mask_all = tile_mask.reshape(N_DOM, TILES_DEV, TILES_DEV)
    halo_all = halo_bonds.reshape(N_DOM, NODE_DEV, ROUNDS * HALO)
    sends = send_rows.reshape(N_DOM, ROUNDS, HALO)
    devices = jnp.arange(N_DOM, dtype=jnp.int32)

    def pick_rows(table, index):
        return table[index]

    def add_rows(table, index, pieces):
        return table.at[index].add(pieces)

    def halo_of(rows):
        pieces = []
        for turn in range(ROUNDS):
            picked = jax.vmap(pick_rows)(rows, sends[:, turn])
            pieces.append(picked[jnp.bitwise_xor(devices, 1 << turn)])
        return jnp.concatenate(pieces, axis=1)

    def local_sum(items):
        bonds, mask, halo_b, rows, halo_rows = items
        tiles = bonds * expand_mask(mask)
        return jnp.dot(tiles, rows, preferred_element_type=jnp.float32) + jnp.dot(halo_b, halo_rows, preferred_element_type=jnp.float32)

    def local_back(items):
        bonds, mask, halo_b, cotan = items
        tiles = bonds * expand_mask(mask)
        return (jnp.dot(tiles.T, cotan, preferred_element_type=jnp.float32), jnp.dot(halo_b.T, cotan, preferred_element_type=jnp.float32))
    feats = features.reshape(N_DOM, NODE_DEV, H)
    first_agg = lax.map(local_sum, (bond_all, mask_all, halo_all, feats, halo_of(feats))).astype(jnp.bfloat16)
    flat_first = first_agg.reshape(NODES, H)
    first_pre = jnp.dot(flat_first, first_weight, preferred_element_type=jnp.float32)
    hidden = (features.astype(jnp.float32) + jax.nn.silu(first_pre)).astype(jnp.bfloat16)
    hid3 = hidden.reshape(N_DOM, NODE_DEV, H)
    second_agg = lax.map(local_sum, (bond_all, mask_all, halo_all, hid3, halo_of(hid3))).astype(jnp.bfloat16)
    flat_second = second_agg.reshape(NODES, H)
    output = hidden.astype(jnp.float32) + jnp.dot(flat_second, second_weight, preferred_element_type=jnp.float32)
    prediction = output.astype(jnp.bfloat16)
    error = (output - targets.astype(jnp.float32)) * (1.0 / math.sqrt(NODES))
    error_b = error.astype(jnp.bfloat16)
    grad_second = jnp.dot(flat_second.T, error_b, preferred_element_type=jnp.float32)
    agg_cot = jnp.dot(error_b, second_weight.T, preferred_element_type=jnp.float32).astype(jnp.bfloat16)
    local_cot, halo_cot = lax.map(local_back, (bond_all, mask_all, halo_all, agg_cot.reshape(N_DOM, NODE_DEV, H)))
    total = jnp.zeros((N_DOM, NODE_DEV, H), jnp.float32)
    for turn in range(ROUNDS):
        block = halo_cot[:, turn * HALO:(turn + 1) * HALO][jnp.bitwise_xor(devices, 1 << turn)]
        total = jax.vmap(add_rows)(total, sends[:, turn], block)
    hidden_cot = error + (local_cot + total).reshape(NODES, H)
    sigm = jax.nn.sigmoid(first_pre)
    pre_cot = (hidden_cot * sigm * (1.0 + first_pre * (1.0 - sigm))).astype(jnp.bfloat16)
    grad_first = jnp.dot(flat_first.T, pre_cot, preferred_element_type=jnp.float32)
    return (prediction, grad_first, grad_second)
```

```python
import functools
import math

import jax
import jax.numpy as jnp
from jax import lax
from jax.experimental import pallas as pl
from jax.experimental.pallas import tpu as pltpu
from jax.sharding import PartitionSpec as P

MESH = pl.DeviceIdType.MESH
ROUNDS = 4
BF = jnp.bfloat16
F32 = jnp.float32


def dot(a, b):
    return jnp.dot(a, b, preferred_element_type=F32)


def dot_rows(a, b):
    return lax.dot_general(a, b, (((0,), (0,)), ((), ())), preferred_element_type=F32)


def dot_lanes(a, b):
    return lax.dot_general(a, b, (((1,), (1,)), ((), ())), preferred_element_type=F32)


def tree(values):
    while len(values) > 1:
        values = [values[i] + values[i + 1] for i in range(0, len(values), 2)]
    return values[0]


def subsets(bits):
    return [[b for j, b in enumerate(bits) if (d >> j) & 1] for d in range(1, 1 << len(bits))]


def body(
    groups, n, nodes,
    feat_h, targ_h, w1_h, w2_h, bonds_h, halo_h, mask_h, send_h,
    pred_h, g1_o, g2_o,
    feat, targ, w1, w2, bonds, halo, mask, send,
    spread, hot, inner, agg1, deriv, hid, agg2, err, err_b, pred,
    out_buf, in_buf, grads, got_z, sum_z, got_y, sum_y, got_x, full,
    load_sem, store_sem, hs_sem, hr_sem, as_sem, ar_sem,
):
    rows, width = feat.shape
    step = 384 if rows % 384 == 0 else 64
    blocks = [pl.ds(i, step) for i in range(0, rows, step)]
    hw = send.shape[1]

    def load(i, a, b):
        copy = pltpu.make_async_copy(a, b, load_sem.at[i])
        copy.start()
        return copy

    c_feat = load(0, feat_h, feat)
    c_send = load(1, send_h, send)
    c_mask = load(2, mask_h, mask)
    c_bonds = load(3, bonds_h, bonds)
    c_halo = load(4, halo_h, halo)
    c_w1 = load(5, w1_h, w1)
    c_w2 = load(6, w2_h, w2)
    c_targ = load(7, targ_h, targ)

    me = lax.axis_index("dom")
    delta = [
        (1 << b) * (1 - 2 * lax.rem(lax.div(me, 1 << b), 2)) for b in range(n.bit_length() - 1)
    ]

    def peer(bits):
        return me + sum(delta[b] for b in bits)

    zb, yb, xb = groups
    peers = [[peer(s) for s in subsets(g)] for g in groups]
    zsize = 1 << len(zb)
    chunk = width // zsize

    def zpos(device):
        return lax.rem(lax.div(device, 1 << zb[0]), zsize)

    barrier = pltpu.get_barrier_semaphore()
    count = 0
    for group in peers:
        for p in group:
            pl.semaphore_signal(barrier, inc=1, device_id=(p,), device_id_type=MESH)
            count += 1

    def remote(src, dst, ss, rs, p):
        return pltpu.make_async_remote_copy(
            src_ref=src, dst_ref=dst, send_sem=ss, recv_sem=rs, device_id=(p,), device_id_type=MESH
        )

    def exchange(k):
        copies = []
        for r in reversed(range(ROUNDS)):
            c = remote(
                out_buf.at[k, pl.ds(r * hw, hw)], in_buf.at[k, pl.ds(r * hw, hw)],
                hs_sem.at[k, r], hr_sem.at[k, r], peer([r]),
            )
            c.start()
            copies.append(c)
        return copies

    c_send.wait()
    for r in range(ROUNDS):
        spot = lax.broadcasted_iota(jnp.int32, (rows, hw), 0)
        hot[:, r * hw : (r + 1) * hw] = (spot == send[r : r + 1, :]).astype(F32).astype(BF)
    c_feat.wait()
    out_buf[0] = dot_rows(hot[...], feat[...]).astype(BF)
    pl.semaphore_wait(barrier, count)
    first = exchange(0)

    c_mask.wait()
    tiles = mask.shape[0]
    tile = rows // tiles
    col = lax.broadcasted_iota(jnp.int32, (tiles, rows), 1)
    total = jnp.zeros((tiles, rows), F32)
    for t in range(tiles):
        inside = (col >= t * tile) & (col < (t + 1) * tile)
        total = total + jnp.where(inside, mask[:, t : t + 1].astype(F32), 0.0)
    spread[...] = total
    c_bonds.wait()
    for t in range(tiles):
        part = pl.ds(t * tile, tile)
        bonds[part, :] = bonds[part, :] * spread[t : t + 1, :].astype(BF)
    for b in blocks:
        inner[b, :] = dot(bonds[b, :], feat[...])
    c_halo.wait()
    c_w1.wait()
    for c in first:
        c.wait_recv()
    for b in blocks:
        a = (inner[b, :] + dot(halo[b, :], in_buf[0])).astype(BF)
        agg1[b, :] = a
        u = dot(a, w1[...])
        s = jax.nn.sigmoid(u)
        hid[b, :] = (feat[b, :].astype(F32) + u * s).astype(BF)
        deriv[b, :] = s * (1.0 + u * (1.0 - s))

    out_buf[1] = dot_rows(hot[...], hid[...]).astype(BF)
    second = exchange(1)
    for b in blocks:
        inner[b, :] = dot(bonds[b, :], hid[...])
    c_w2.wait()
    c_targ.wait()
    for c in second:
        c.wait_recv()
    scale = 1.0 / math.sqrt(nodes)
    for b in blocks:
        a = (inner[b, :] + dot(halo[b, :], in_buf[1])).astype(BF)
        agg2[b, :] = a
        o = hid[b, :].astype(F32) + dot(a, w2[...])
        pred[b, :] = o.astype(BF)
        e = (o - targ[b, :].astype(F32)) * scale
        err[b, :] = e
        err_b[b, :] = e.astype(BF)
    c_pred = pltpu.make_async_copy(pred, pred_h, store_sem)
    c_pred.start()

    cot = dot_lanes(w2[...], err_b[...]).astype(BF)
    back = dot(cot, halo[...]).astype(BF)
    for r in range(ROUNDS):
        out_buf[2, r * hw : (r + 1) * hw, :] = back[:, r * hw : (r + 1) * hw].astype(F32).T.astype(BF)
    third = exchange(2)

    def all_of(k, phase, ref):
        return remote(ref, ref, as_sem.at[k, phase], ar_sem.at[k, phase], peers[0][0])

    def reduce_z(k):
        for i, p in enumerate(peers[0]):
            start = pl.multiple_of(zpos(p) * chunk, chunk)
            remote(
                grads.at[k, pl.ds(start, chunk)], got_z.at[k, i], as_sem.at[k, 0], ar_sem.at[k, 0], p
            ).start()

    def reduce_y(k):
        all_of(k, 0, got_z.at[k]).wait_recv()
        mine = pl.multiple_of(zpos(me) * chunk, chunk)
        own = grads[k, pl.ds(mine, chunk), :]
        sum_z[k] = tree([own] + [got_z[k, i] for i in range(len(peers[0]))])
        for i, p in enumerate(peers[1]):
            remote(sum_z.at[k], got_y.at[k, i], as_sem.at[k, 1], ar_sem.at[k, 1], p).start()

    def reduce_x(k):
        all_of(k, 1, got_y.at[k]).wait_recv()
        sum_y[k] = tree([sum_z[k]] + [got_y[k, i] for i in range(len(peers[1]))])
        for i, p in enumerate(peers[2]):
            remote(sum_y.at[k], got_x.at[k, i], as_sem.at[k, 2], ar_sem.at[k, 2], p).start()

    def gather_z(k):
        all_of(k, 2, got_x.at[k]).wait_recv()
        mine = pl.multiple_of(zpos(me) * chunk, chunk)
        here = full.at[k, pl.ds(mine, chunk)]
        full[k, pl.ds(mine, chunk), :] = tree([sum_y[k]] + [got_x[k, i] for i in range(len(peers[2]))])
        for p in peers[0]:
            remote(here, here, as_sem.at[k, 3], ar_sem.at[k, 3], p).start()

    def finish(k, out):
        all_of(k, 3, full.at[k, pl.ds(0, width - chunk)]).wait_recv()
        out[...] = full[k]
        all_of(k, 0, got_z.at[k]).wait_send()
        all_of(k, 1, got_y.at[k]).wait_send()
        all_of(k, 2, got_x.at[k]).wait_send()
        all_of(k, 3, full.at[k, pl.ds(0, width - chunk)]).wait_send()

    grads[0] = dot_rows(agg2[...], err_b[...])
    reduce_z(0)
    inner[...] = dot(cot, bonds[...]).T
    reduce_y(0)
    for c in third:
        c.wait_recv()
    pre = []
    for b in blocks:
        h = err[b, :] + inner[b, :] + dot(hot[b, :], in_buf[2])
        hid[b, :] = (h * deriv[b, :]).astype(BF)
    grads[1] = dot_rows(agg1[...], hid[...])
    reduce_z(1)
    reduce_x(0)
    reduce_y(1)
    gather_z(0)
    reduce_x(1)
    finish(0, g2_o)
    gather_z(1)
    finish(1, g1_o)
    for c in first + second + third:
        c.wait_send()
    c_pred.wait()


def make_local(n, groups):
    def local(features, targets, first_weight, second_weight, local_bonds, halo_bonds, tile_mask, send_rows):
        rows, width = features.shape
        hw = ROUNDS * send_rows.shape[1]
        zs, ys, xs = (1 << len(g) for g in groups)
        chunk = width // zs
        hbm = pl.BlockSpec(memory_space=pl.ANY)
        vmem = pl.BlockSpec(memory_space=pltpu.VMEM)
        args = (features, targets, first_weight, second_weight, local_bonds, halo_bonds, tile_mask, send_rows)
        tiles = tile_mask.shape[0]
        return pl.pallas_call(
            functools.partial(body, groups, n, rows * n),
            out_shape=(
                jax.ShapeDtypeStruct((rows, width), BF),
                jax.ShapeDtypeStruct((width, width), F32),
                jax.ShapeDtypeStruct((width, width), F32),
            ),
            in_specs=[hbm] * 8,
            out_specs=(hbm, vmem, vmem),
            scratch_shapes=[pltpu.VMEM(a.shape, a.dtype) for a in args]
            + [
                pltpu.VMEM((tiles, rows), F32),
                pltpu.VMEM((rows, hw), BF),
                pltpu.VMEM((rows, width), F32),
                pltpu.VMEM((rows, width), BF),
                pltpu.VMEM((rows, width), F32),
                pltpu.VMEM((rows, width), BF),
                pltpu.VMEM((rows, width), BF),
                pltpu.VMEM((rows, width), F32),
                pltpu.VMEM((rows, width), BF),
                pltpu.VMEM((rows, width), BF),
                pltpu.VMEM((3, hw, width), BF),
                pltpu.VMEM((3, hw, width), BF),
                pltpu.VMEM((2, width, width), F32),
                pltpu.VMEM((2, zs - 1, chunk, width), F32),
                pltpu.VMEM((2, chunk, width), F32),
                pltpu.VMEM((2, ys - 1, chunk, width), F32),
                pltpu.VMEM((2, chunk, width), F32),
                pltpu.VMEM((2, xs - 1, chunk, width), F32),
                pltpu.VMEM((2, width, width), F32),
                pltpu.SemaphoreType.DMA((8,)),
                pltpu.SemaphoreType.DMA,
                pltpu.SemaphoreType.DMA((3, ROUNDS)),
                pltpu.SemaphoreType.DMA((3, ROUNDS)),
                pltpu.SemaphoreType.DMA((2, 4)),
                pltpu.SemaphoreType.DMA((2, 4)),
            ],
            compiler_params=pltpu.CompilerParams(collective_id=0, has_side_effects=True),
            name="step",
        )(*args)

    return local


def solution(mesh):
    n = mesh.shape["dom"]
    groups = ((1, 2, 3), (4, 5, 6), (0, 7, 8)) if n == 512 else ((1, 2), (3,), (0,))
    split = P("dom", None)
    return jax.shard_map(
        make_local(n, groups),
        mesh=mesh,
        in_specs=(split, split, P(), P(), split, split, split, split),
        out_specs=(split, P(), P()),
        check_vma=False,
    )
```

```python
import functools
import math

import jax
import jax.numpy as jnp
from jax import lax
from jax.experimental import pallas as pl
from jax.experimental.pallas import tpu as pltpu
from jax.sharding import PartitionSpec as P

MESH = pl.DeviceIdType.MESH
ROUNDS = 4
BF = jnp.bfloat16
F32 = jnp.float32
NEAR, YAXIS, ZAXIS = (0, 7, 8), (4, 5, 6), (1, 2, 3)
ORDERS = ((NEAR, YAXIS, ZAXIS), (NEAR, ZAXIS, YAXIS))
GROUP = 8


def dot(a, b):
    return jnp.dot(a, b, preferred_element_type=F32)


def tree(values):
    while len(values) > 1:
        values = [values[i] + values[i + 1] for i in range(0, len(values), 2)]
    return values[0]


def body(
    nodes,
    feat_h, targ_h, w1_h, w2_h, bonds_h, halo_h, mask_h, send_h,
    pred, grads_o,
    feat, targ, w1, w2, bonds, halo, mask, send,
    spread, hot, inner, agg1, hid, hid_far, agg2, err_t, err_bt, slope_t, slope_far_t,
    out_buf, in_buf, grads, got, part, full,
    load_sem, hs_sem, hr_sem, as_sem, ar_sem,
):
    rows, width = feat.shape
    step = 384
    blocks = [pl.ds(i, step) for i in range(0, rows, step)]
    hw = send.shape[1]
    chunk = width // GROUP

    def load(i, a, b):
        copy = pltpu.make_async_copy(a, b, load_sem.at[i])
        copy.start()
        return copy

    c_send = load(1, send_h, send)
    c_feat = load(0, feat_h, feat)
    c_mask = load(2, mask_h, mask)
    c_bonds = load(3, bonds_h, bonds)
    c_halo = load(4, halo_h, halo)
    c_w1 = load(5, w1_h, w1)
    c_w2 = load(6, w2_h, w2)
    c_targ = load(7, targ_h, targ)

    me = lax.axis_index("dom")
    delta = [(1 << b) * (1 - 2 * lax.rem(lax.div(me, 1 << b), 2)) for b in range(9)]

    def peers(bits):
        return [
            me + sum(delta[b] for j, b in enumerate(bits) if (d >> j) & 1) for d in range(1, GROUP)
        ]

    groups = {bits: peers(bits) for bits in (NEAR, YAXIS, ZAXIS)}

    def place(device):
        return pl.multiple_of((lax.rem(device, 2) + 2 * lax.div(device, 128)) * chunk, chunk)

    barrier = pltpu.get_barrier_semaphore()
    for group in groups.values():
        for p in group:
            pl.semaphore_signal(barrier, inc=1, device_id=(p,), device_id_type=MESH)

    def remote(src, dst, ss, rs, p):
        return pltpu.make_async_remote_copy(
            src_ref=src, dst_ref=dst, send_sem=ss, recv_sem=rs, device_id=(p,), device_id_type=MESH
        )

    def exchange(k):
        copies = []
        for r in reversed(range(ROUNDS)):
            c = remote(
                out_buf.at[k, pl.ds(r * hw, hw)], in_buf.at[k, pl.ds(r * hw, hw)],
                hs_sem.at[k, r], hr_sem.at[k, r], me + delta[r],
            )
            c.start()
            copies.append(c)
        return copies

    c_send.wait()
    for r in range(ROUNDS):
        wanted = jnp.broadcast_to(send[r : r + 1, :].astype(F32), (hw, hw)).T.astype(jnp.int32)
        lane = lax.broadcasted_iota(jnp.int32, (hw, hw), 1)
        for c in range(0, rows, hw):
            hot[r * hw : (r + 1) * hw, c : c + hw] = (wanted == lane + c).astype(F32).astype(BF)
    c_feat.wait()
    out_buf[0] = dot(hot[...], feat[...]).astype(BF)
    pl.semaphore_wait(barrier, 3 * (GROUP - 1))
    first = exchange(0)

    c_mask.wait()
    tiles = mask.shape[0]
    tile = rows // tiles
    col = lax.broadcasted_iota(jnp.int32, (tiles, rows), 1)
    total = jnp.zeros((tiles, rows), F32)
    for t in range(tiles):
        inside = (col >= t * tile) & (col < (t + 1) * tile)
        total = total + jnp.where(inside, mask[:, t : t + 1].astype(F32), 0.0)
    spread[...] = total
    c_bonds.wait()
    for t in range(tiles):
        here = pl.ds(t * tile, tile)
        bonds[here, :] = bonds[here, :] * spread[t : t + 1, :].astype(BF)
    for b in blocks:
        inner[b, :] = dot(bonds[b, :], feat[...])
    c_halo.wait()
    c_w1.wait()
    for c in first:
        c.wait_recv()
    for b in blocks:
        agg1[b, :] = (inner[b, :] + dot(halo[b, :], in_buf[0])).astype(BF)

    out_buf[1] = dot(hot[...], agg1[...]).astype(BF)
    second = exchange(1)

    def activate(a, x):
        u = dot(a, w1[...])
        s = jax.nn.sigmoid(u)
        return (x.astype(F32) + u * s).astype(BF), s * (1.0 + u * (1.0 - s))

    for i in range(0, rows, step):
        b = pl.ds(i, step)
        hid[b, :], slope = activate(agg1[b, :], feat[b, :])
        slope_t[:, i : i + step] = slope.T
    for b in blocks:
        inner[b, :] = dot(bonds[b, :], hid[...])
    c_w2.wait()
    c_targ.wait()
    for c in second:
        c.wait_recv()
    hid_far[...], slope = activate(in_buf[1], in_buf[0])
    slope_far_t[...] = slope.T
    scale = 1.0 / math.sqrt(nodes)
    for i in range(0, rows, step):
        b = pl.ds(i, step)
        a = (inner[b, :] + dot(halo[b, :], hid_far[...])).astype(BF)
        agg2[b, :] = a
        o = hid[b, :].astype(F32) + dot(a, w2[...])
        pred[b, :] = o.astype(BF)
        e = ((o - targ[b, :].astype(F32)) * scale).T
        err_t[:, i : i + step] = e
        err_bt[:, i : i + step] = e.astype(BF)

    def all_of(k, phase, ref):
        return remote(ref, ref, as_sem.at[k, phase], ar_sem.at[k, phase], groups[NEAR][0])

    def split(k):
        for i, p in enumerate(groups[ORDERS[k][0]]):
            remote(
                grads.at[k, pl.ds(place(p), chunk)], got.at[k, 0, i], as_sem.at[k, 0], ar_sem.at[k, 0], p
            ).start()

    def add(k, phase):
        all_of(k, phase, got.at[k, phase]).wait_recv()
        own = grads[k, pl.ds(place(me), chunk), :] if phase == 0 else part[k, phase - 1]
        return tree([own] + [got[k, phase, i] for i in range(GROUP - 1)])

    def share(k, phase):
        part[k, phase] = add(k, phase)
        for i, p in enumerate(groups[ORDERS[k][phase + 1]]):
            remote(
                part.at[k, phase], got.at[k, phase + 1, i],
                as_sem.at[k, phase + 1], ar_sem.at[k, phase + 1], p,
            ).start()

    def gather(k):
        here = full.at[k, pl.ds(place(me), chunk)]
        full[k, pl.ds(place(me), chunk), :] = add(k, 2)
        for p in groups[NEAR]:
            remote(here, here, as_sem.at[k, 3], ar_sem.at[k, 3], p).start()

    def finish(k):
        rest = full.at[k, pl.ds(0, width - chunk)]
        all_of(k, 3, rest).wait_recv()
        grads_o[k] = full[k]
        for phase in range(3):
            all_of(k, phase, got.at[k, phase]).wait_send()
        all_of(k, 3, rest).wait_send()

    grads[0] = dot(err_bt[...], agg2[...])
    split(0)
    cot = dot(w2[...], err_bt[...]).astype(BF)
    near = ((err_t[...] + dot(cot, bonds[...])) * slope_t[...]).astype(BF)
    far = (dot(cot, halo[...]) * slope_far_t[...]).astype(BF)
    grads[1] = dot(near, agg1[...]) + dot(far, in_buf[1])
    split(1)
    for phase in range(2):
        share(0, phase)
        share(1, phase)
    gather(0)
    gather(1)
    for c in first + second:
        c.wait_send()
    finish(0)
    finish(1)


def write_out(pred_i, grads_i, pred_o, g1_o, g2_o):
    pred_o[...] = pred_i[...]
    g2_o[...] = grads_i[0].T
    g1_o[...] = grads_i[1].T


def make_local(n):
    def local(features, targets, first_weight, second_weight, local_bonds, halo_bonds, tile_mask, send_rows):
        rows, width = features.shape
        hw = ROUNDS * send_rows.shape[1]
        chunk = width // GROUP
        hbm = pl.BlockSpec(memory_space=pltpu.HBM)
        vmem = pl.BlockSpec(memory_space=pltpu.VMEM)
        args = (features, targets, first_weight, second_weight, local_bonds, halo_bonds, tile_mask, send_rows)
        pred, grads = pl.pallas_call(
            functools.partial(body, rows * n),
            out_shape=(
                pltpu.VMEM((rows, width), BF),
                pltpu.VMEM((2, width, width), F32),
            ),
            in_specs=[hbm] * 8,
            out_specs=(vmem, vmem),
            scratch_shapes=[pltpu.VMEM(a.shape, a.dtype) for a in args]
            + [
                pltpu.VMEM((tile_mask.shape[0], rows), F32),
                pltpu.VMEM((hw, rows), BF),
                pltpu.VMEM((rows, width), F32),
                pltpu.VMEM((rows, width), BF),
                pltpu.VMEM((rows, width), BF),
                pltpu.VMEM((hw, width), BF),
                pltpu.VMEM((rows, width), BF),
                pltpu.VMEM((width, rows), F32),
                pltpu.VMEM((width, rows), BF),
                pltpu.VMEM((width, rows), F32),
                pltpu.VMEM((width, hw), F32),
                pltpu.VMEM((2, hw, width), BF),
                pltpu.VMEM((2, hw, width), BF),
                pltpu.VMEM((2, width, width), F32),
                pltpu.VMEM((2, 3, GROUP - 1, chunk, width), F32),
                pltpu.VMEM((2, 2, chunk, width), F32),
                pltpu.VMEM((2, width, width), F32),
                pltpu.SemaphoreType.DMA((8,)),
                pltpu.SemaphoreType.DMA((2, ROUNDS)),
                pltpu.SemaphoreType.DMA((2, ROUNDS)),
                pltpu.SemaphoreType.DMA((2, 4)),
                pltpu.SemaphoreType.DMA((2, 4)),
            ],
            compiler_params=pltpu.CompilerParams(
                collective_id=0, has_side_effects=True,
            ),
            name="step",
        )(*args)
        return pl.pallas_call(
            write_out,
            out_shape=(
                jax.ShapeDtypeStruct((rows, width), BF),
                jax.ShapeDtypeStruct((width, width), F32),
                jax.ShapeDtypeStruct((width, width), F32),
            ),
            in_specs=[vmem] * 2,
            out_specs=(vmem, vmem, vmem),
            compiler_params=pltpu.CompilerParams(vmem_limit_bytes=4 << 20),
            name="write_out",
        )(pred, grads)

    return local


def solution(mesh):
    split = P("dom", None)
    return jax.shard_map(
        make_local(mesh.shape["dom"]),
        mesh=mesh,
        in_specs=(split, split, P(), P(), split, split, split, split),
        out_specs=(split, P(), P()),
        check_vma=False,
    )
```

```python
import functools
import math

import jax
import jax.numpy as jnp
from jax import lax
from jax.experimental import pallas as pl
from jax.experimental.pallas import tpu as pltpu
from jax.sharding import PartitionSpec as P

MESH = pl.DeviceIdType.MESH
ROUNDS = 4
BF = jnp.bfloat16
F32 = jnp.float32
NEAR, YAXIS, ZAXIS = (0, 7, 8), (4, 5, 6), (1, 2, 3)
ORDERS = ((NEAR, YAXIS, ZAXIS), (NEAR, ZAXIS, YAXIS))
GROUP = 8
FAR_FIRST = (4, 5, 3, 7, 6, 2, 1)


def dot(a, b):
    return jnp.dot(a, b, preferred_element_type=F32)


def tree(values):
    while len(values) > 1:
        values = [values[i] + values[i + 1] for i in range(0, len(values), 2)]
    return values[0]


def body(
    nodes,
    feat_h, targ_h, w1_h, w2_h, bonds_h, halo_h, mask_h, send_h,
    pred, grads_o,
    feat, targ, w1, w2, bonds, halo, mask, send,
    spread, hot, halves, halo_sent, sent, inner, agg1, hid, hid_far, agg2, err_t, err_bt, slope_t, slope_far_t,
    out_buf, in_buf, grads, got, part, full,
    load_sem, hs_sem, hr_sem, as_sem, ar_sem,
):
    rows, width = feat.shape
    step = 384
    blocks = [pl.ds(i, step) for i in range(0, rows, step)]
    hw = send.shape[1]
    chunk = width // GROUP

    def load(i, a, b):
        copy = pltpu.make_async_copy(a, b, load_sem.at[i])
        copy.start()
        return copy

    c_send = load(1, send_h, send)
    c_feat = load(0, feat_h, feat)
    c_mask = load(2, mask_h, mask)
    c_bonds = load(3, bonds_h, bonds)
    c_halo = load(4, halo_h, halo)
    c_w1 = load(5, w1_h, w1)
    c_w2 = load(6, w2_h, w2)
    c_targ = load(7, targ_h, targ)

    me = lax.axis_index("dom")
    delta = [(1 << b) * (1 - 2 * lax.rem(lax.div(me, 1 << b), 2)) for b in range(9)]

    def peers(bits):
        return [
            me + sum(delta[b] for j, b in enumerate(bits) if (d >> j) & 1) for d in FAR_FIRST
        ]

    groups = {bits: peers(bits) for bits in (NEAR, YAXIS, ZAXIS)}

    def place(device):
        return pl.multiple_of((lax.rem(device, 2) + 2 * lax.div(device, 128)) * chunk, chunk)

    barrier = pltpu.get_barrier_semaphore()
    for bits in (ZAXIS, YAXIS, NEAR):
        for p in groups[bits]:
            pl.semaphore_signal(barrier, inc=1, device_id=(p,), device_id_type=MESH)

    def remote(src, dst, ss, rs, p):
        return pltpu.make_async_remote_copy(
            src_ref=src, dst_ref=dst, send_sem=ss, recv_sem=rs, device_id=(p,), device_id_type=MESH
        )

    def exchange(k):
        copies = []
        for r in reversed(range(ROUNDS)):
            c = remote(
                out_buf.at[k, pl.ds(r * hw, hw)], in_buf.at[k, pl.ds(r * hw, hw)],
                hs_sem.at[k, r], hr_sem.at[k, r], me + delta[r],
            )
            c.start()
            copies.append(c)
        return copies

    c_send.wait()
    for r in range(ROUNDS):
        wanted = jnp.broadcast_to(send[r : r + 1, :].astype(F32), (hw, hw)).T.astype(jnp.int32)
        lane = lax.broadcasted_iota(jnp.int32, (hw, hw), 1)
        for c in range(0, rows, hw):
            hot[r * hw : (r + 1) * hw, c : c + hw] = (wanted == lane + c).astype(F32).astype(BF)
    c_feat.wait()
    out_buf[0] = dot(hot[...], feat[...]).astype(BF)

    c_mask.wait()
    tiles = mask.shape[0]
    tile = rows // tiles
    col = lax.broadcasted_iota(jnp.int32, (tiles, rows), 1)
    total = jnp.zeros((tiles, rows), F32)
    for t in range(tiles):
        inside = (col >= t * tile) & (col < (t + 1) * tile)
        total = total + jnp.where(inside, mask[:, t : t + 1].astype(F32), 0.0)
    spread[...] = total
    c_bonds.wait()
    for t in range(tiles):
        here = pl.ds(t * tile, tile)
        bonds[here, :] = bonds[here, :] * spread[t : t + 1, :].astype(BF)
    pl.semaphore_wait(barrier, 3 * (GROUP - 1))
    first = exchange(0)

    for b in blocks:
        v = dot(bonds[b, :], feat[...])
        inner[b, :] = v
        high = v.astype(BF)
        halves[b, :width] = high
        halves[b, width:] = (v - high.astype(F32)).astype(BF)
    c_halo.wait()
    halo_sent[...] = dot(hot[...], halo[...]).astype(BF)
    both = dot(hot[...], halves[...])
    sent[...] = both[:, :width] + both[:, width:]
    c_w1.wait()
    last = (ROUNDS - 1) * hw
    for c in first[1:]:
        c.wait_recv()
    sent[...] += dot(halo_sent[:, :last], in_buf[0, :last, :])
    first[0].wait_recv()

    out_buf[1] = (sent[...] + dot(halo_sent[:, last:], in_buf[0, last:, :])).astype(BF)
    second = exchange(1)

    def activate(a, x):
        u = dot(a, w1[...])
        s = jax.nn.sigmoid(u)
        return (x.astype(F32) + u * s).astype(BF), s * (1.0 + u * (1.0 - s))

    for i in range(0, rows, step):
        b = pl.ds(i, step)
        a = (inner[b, :] + dot(halo[b, :], in_buf[0])).astype(BF)
        agg1[b, :] = a
        hid[b, :], slope = activate(a, feat[b, :])
        slope_t[:, i : i + step] = slope.T
    c_w2.wait()
    c_targ.wait()
    for c in second[1:]:
        c.wait_recv()
    hid_far[:last, :], slope = activate(in_buf[1, :last, :], in_buf[0, :last, :])
    slope_far_t[:, :last] = slope.T
    for b in blocks:
        inner[b, :] = dot(bonds[b, :], hid[...]) + dot(halo[b, :last], hid_far[:last, :])
    second[0].wait_recv()
    hid_far[last:, :], slope = activate(in_buf[1, last:, :], in_buf[0, last:, :])
    slope_far_t[:, last:] = slope.T
    scale = 1.0 / math.sqrt(nodes)
    for i in range(0, rows, step):
        b = pl.ds(i, step)
        a = (inner[b, :] + dot(halo[b, last:], hid_far[last:, :])).astype(BF)
        agg2[b, :] = a
        o = hid[b, :].astype(F32) + dot(a, w2[...])
        pred[b, :] = o.astype(BF)
        e = ((o - targ[b, :].astype(F32)) * scale).T
        err_t[:, i : i + step] = e
        err_bt[:, i : i + step] = e.astype(BF)

    def all_of(k, phase, ref):
        return remote(ref, ref, as_sem.at[k, phase], ar_sem.at[k, phase], groups[NEAR][0])

    def split(k):
        for i, p in enumerate(groups[ORDERS[k][0]]):
            remote(
                grads.at[k, pl.ds(place(p), chunk)], got.at[k, 0, i], as_sem.at[k, 0], ar_sem.at[k, 0], p
            ).start()

    def add(k, phase):
        all_of(k, phase, got.at[k, phase]).wait_recv()
        own = grads[k, pl.ds(place(me), chunk), :] if phase == 0 else part[k, phase - 1]
        return tree([own] + [got[k, phase, FAR_FIRST.index(d)] for d in range(1, GROUP)])

    def share(k, phase):
        part[k, phase] = add(k, phase)
        for i, p in enumerate(groups[ORDERS[k][phase + 1]]):
            remote(
                part.at[k, phase], got.at[k, phase + 1, i],
                as_sem.at[k, phase + 1], ar_sem.at[k, phase + 1], p,
            ).start()

    def gather(k):
        here = full.at[k, pl.ds(place(me), chunk)]
        full[k, pl.ds(place(me), chunk), :] = add(k, 2)
        for p in groups[NEAR]:
            remote(here, here, as_sem.at[k, 3], ar_sem.at[k, 3], p).start()

    def finish(k):
        rest = full.at[k, pl.ds(0, width - chunk)]
        all_of(k, 3, rest).wait_recv()
        grads_o[k] = full[k]
        for phase in range(3):
            all_of(k, phase, got.at[k, phase]).wait_send()
        all_of(k, 3, rest).wait_send()

    grads[0] = dot(err_bt[...], agg2[...])
    split(0)
    cot = dot(w2[...], err_bt[...]).astype(BF)
    near = ((err_t[...] + dot(cot, bonds[...])) * slope_t[...]).astype(BF)
    far = (dot(cot, halo[...]) * slope_far_t[...]).astype(BF)
    grads[1] = dot(near, agg1[...]) + dot(far, in_buf[1])
    split(1)
    for phase in range(2):
        share(0, phase)
        share(1, phase)
    gather(0)
    gather(1)
    for c in first + second:
        c.wait_send()
    finish(0)
    finish(1)


def write_out(pred_i, grads_i, pred_o, g1_o, g2_o):
    pred_o[...] = pred_i[...]
    g2_o[...] = grads_i[0].T
    g1_o[...] = grads_i[1].T


def make_local(n):
    def local(features, targets, first_weight, second_weight, local_bonds, halo_bonds, tile_mask, send_rows):
        rows, width = features.shape
        hw = ROUNDS * send_rows.shape[1]
        chunk = width // GROUP
        hbm = pl.BlockSpec(memory_space=pltpu.HBM)
        vmem = pl.BlockSpec(memory_space=pltpu.VMEM)
        args = (features, targets, first_weight, second_weight, local_bonds, halo_bonds, tile_mask, send_rows)
        pred, grads = pl.pallas_call(
            functools.partial(body, rows * n),
            out_shape=(
                pltpu.VMEM((rows, width), BF),
                pltpu.VMEM((2, width, width), F32),
            ),
            in_specs=[hbm] * 8,
            out_specs=(vmem, vmem),
            scratch_shapes=[pltpu.VMEM(a.shape, a.dtype) for a in args]
            + [
                pltpu.VMEM((tile_mask.shape[0], rows), F32),
                pltpu.VMEM((hw, rows), BF),
                pltpu.VMEM((rows, 2 * width), BF),
                pltpu.VMEM((hw, hw), BF),
                pltpu.VMEM((hw, width), F32),
                pltpu.VMEM((rows, width), F32),
                pltpu.VMEM((rows, width), BF),
                pltpu.VMEM((rows, width), BF),
                pltpu.VMEM((hw, width), BF),
                pltpu.VMEM((rows, width), BF),
                pltpu.VMEM((width, rows), F32),
                pltpu.VMEM((width, rows), BF),
                pltpu.VMEM((width, rows), F32),
                pltpu.VMEM((width, hw), F32),
                pltpu.VMEM((2, hw, width), BF),
                pltpu.VMEM((2, hw, width), BF),
                pltpu.VMEM((2, width, width), F32),
                pltpu.VMEM((2, 3, GROUP - 1, chunk, width), F32),
                pltpu.VMEM((2, 2, chunk, width), F32),
                pltpu.VMEM((2, width, width), F32),
                pltpu.SemaphoreType.DMA((8,)),
                pltpu.SemaphoreType.DMA((2, ROUNDS)),
                pltpu.SemaphoreType.DMA((2, ROUNDS)),
                pltpu.SemaphoreType.DMA((2, 4)),
                pltpu.SemaphoreType.DMA((2, 4)),
            ],
            compiler_params=pltpu.CompilerParams(
                collective_id=0, has_side_effects=True,
            ),
            name="step",
        )(*args)
        return pl.pallas_call(
            write_out,
            out_shape=(
                jax.ShapeDtypeStruct((rows, width), BF),
                jax.ShapeDtypeStruct((width, width), F32),
                jax.ShapeDtypeStruct((width, width), F32),
            ),
            in_specs=[vmem] * 2,
            out_specs=(vmem, vmem, vmem),
            compiler_params=pltpu.CompilerParams(vmem_limit_bytes=4 << 20),
            name="write_out",
        )(pred, grads)

    return local


def solution(mesh):
    split = P("dom", None)
    return jax.shard_map(
        make_local(mesh.shape["dom"]),
        mesh=mesh,
        in_specs=(split, split, P(), P(), split, split, split, split),
        out_specs=(split, P(), P()),
        check_vma=False,
    )
```

```python
import functools
import math

import jax
import jax.numpy as jnp
from jax import lax
from jax.experimental import pallas as pl
from jax.experimental.pallas import tpu as pltpu
from jax.sharding import PartitionSpec as P

MESH = pl.DeviceIdType.MESH
ROUNDS = 4
BF = jnp.bfloat16
F32 = jnp.float32
NEAR, YAXIS, ZAXIS = (0, 7, 8), (4, 5, 6), (1, 2, 3)
ORDERS = ((NEAR, YAXIS, ZAXIS), (NEAR, ZAXIS, YAXIS))
GROUP = 8
FAR_FIRST = (4, 5, 3, 7, 6, 2, 1)


def dot(a, b):
    return jnp.dot(a, b, preferred_element_type=F32)


def tree(values):
    while len(values) > 1:
        values = [values[i] + values[i + 1] for i in range(0, len(values), 2)]
    return values[0]


def body(
    nodes,
    feat_h, targ_h, w1_h, w2_h, bonds_h, halo_h, mask_h, send_h,
    pred, grads_o,
    feat, targ, w1, w2, bonds, halo, mask, send,
    spread, hot, halves, halo_sent, sent, inner, agg1, hid, hid_far, agg2, err_t, err_bt, slope_t, slope_far_t,
    out_buf, in_buf, grads, got, part, full,
    load_sem, hs_sem, hr_sem, as_sem, ar_sem,
):
    rows, width = feat.shape
    step = 384
    blocks = [pl.ds(i, step) for i in range(0, rows, step)]
    hw = send.shape[1]
    chunk = width // GROUP

    def load(i, a, b):
        copy = pltpu.make_async_copy(a, b, load_sem.at[i])
        copy.start()
        return copy

    c_send = load(1, send_h, send)
    c_feat = load(0, feat_h, feat)
    c_mask = load(2, mask_h, mask)
    c_bonds = load(3, bonds_h, bonds)
    c_halo = load(4, halo_h, halo)
    c_w1 = load(5, w1_h, w1)
    c_w2 = load(6, w2_h, w2)
    c_targ = load(7, targ_h, targ)

    me = lax.axis_index("dom")
    delta = [(1 << b) * (1 - 2 * lax.rem(lax.div(me, 1 << b), 2)) for b in range(9)]

    def peers(bits):
        return [
            me + sum(delta[b] for j, b in enumerate(bits) if (d >> j) & 1) for d in FAR_FIRST
        ]

    groups = {bits: peers(bits) for bits in (NEAR, YAXIS, ZAXIS)}

    def place(device):
        return pl.multiple_of((lax.rem(device, 2) + 2 * lax.div(device, 128)) * chunk, chunk)

    barrier = pltpu.get_barrier_semaphore()
    for bits in (ZAXIS, YAXIS, NEAR):
        for p in groups[bits]:
            pl.semaphore_signal(barrier, inc=1, device_id=(p,), device_id_type=MESH)

    def remote(src, dst, ss, rs, p):
        return pltpu.make_async_remote_copy(
            src_ref=src, dst_ref=dst, send_sem=ss, recv_sem=rs, device_id=(p,), device_id_type=MESH
        )

    def pass_on(k, r):
        c = remote(
            out_buf.at[k, pl.ds(r * hw, hw)], in_buf.at[k, pl.ds(r * hw, hw)],
            hs_sem.at[k, r], hr_sem.at[k, r], me + delta[r],
        )
        c.start()
        return c

    c_send.wait()
    for r in range(ROUNDS):
        wanted = jnp.broadcast_to(send[r : r + 1, :].astype(F32), (hw, hw)).T.astype(jnp.int32)
        lane = lax.broadcasted_iota(jnp.int32, (hw, hw), 1)
        for c in range(0, rows, hw):
            hot[r * hw : (r + 1) * hw, c : c + hw] = (wanted == lane + c).astype(F32).astype(BF)
    c_feat.wait()
    out_buf[0] = dot(hot[...], feat[...]).astype(BF)

    c_mask.wait()
    tiles = mask.shape[0]
    tile = rows // tiles
    col = lax.broadcasted_iota(jnp.int32, (tiles, rows), 1)
    total = jnp.zeros((tiles, rows), F32)
    for t in range(tiles):
        inside = (col >= t * tile) & (col < (t + 1) * tile)
        total = total + jnp.where(inside, mask[:, t : t + 1].astype(F32), 0.0)
    spread[...] = total
    c_bonds.wait()
    for t in range(tiles):
        here = pl.ds(t * tile, tile)
        bonds[here, :] = bonds[here, :] * spread[t : t + 1, :].astype(BF)
    pl.semaphore_wait(barrier, 3 * (GROUP - 1))
    first = [pass_on(0, ROUNDS - 1)]

    for b in blocks:
        v = dot(bonds[b, :], feat[...])
        inner[b, :] = v
        high = v.astype(BF)
        halves[b, :width] = high
        halves[b, width:] = (v - high.astype(F32)).astype(BF)
    first += [pass_on(0, r) for r in reversed(range(ROUNDS - 1))]
    c_halo.wait()
    halo_sent[...] = dot(hot[...], halo[...]).astype(BF)
    both = dot(hot[...], halves[...])
    sent[...] = both[:, :width] + both[:, width:]
    c_w1.wait()
    last = (ROUNDS - 1) * hw
    for c in first[1:]:
        c.wait_recv()
    sent[...] += dot(halo_sent[:, :last], in_buf[0, :last, :])
    first[0].wait_recv()

    out_buf[1, last:, :] = (sent[last:, :] + dot(halo_sent[last:, last:], in_buf[0, last:, :])).astype(BF)
    second = [pass_on(1, ROUNDS - 1)]
    out_buf[1, :last, :] = (sent[:last, :] + dot(halo_sent[:last, last:], in_buf[0, last:, :])).astype(BF)

    def activate(a, x):
        u = dot(a, w1[...])
        s = jax.nn.sigmoid(u)
        return (x.astype(F32) + u * s).astype(BF), s * (1.0 + u * (1.0 - s))

    for i in range(0, rows, step):
        b = pl.ds(i, step)
        a = (inner[b, :] + dot(halo[b, :], in_buf[0])).astype(BF)
        agg1[b, :] = a
        hid[b, :], slope = activate(a, feat[b, :])
        slope_t[:, i : i + step] = slope.T
        if i == 0:
            second += [pass_on(1, r) for r in reversed(range(ROUNDS - 1))]
    c_w2.wait()
    c_targ.wait()
    for c in second[1:]:
        c.wait_recv()
    hid_far[:last, :], slope = activate(in_buf[1, :last, :], in_buf[0, :last, :])
    slope_far_t[:, :last] = slope.T
    for b in blocks:
        inner[b, :] = dot(bonds[b, :], hid[...]) + dot(halo[b, :last], hid_far[:last, :])
    second[0].wait_recv()
    hid_far[last:, :], slope = activate(in_buf[1, last:, :], in_buf[0, last:, :])
    slope_far_t[:, last:] = slope.T
    scale = 1.0 / math.sqrt(nodes)
    for i in range(0, rows, step):
        b = pl.ds(i, step)
        a = (inner[b, :] + dot(halo[b, last:], hid_far[last:, :])).astype(BF)
        agg2[b, :] = a
        o = hid[b, :].astype(F32) + dot(a, w2[...])
        pred[b, :] = o.astype(BF)
        e = ((o - targ[b, :].astype(F32)) * scale).T
        err_t[:, i : i + step] = e
        err_bt[:, i : i + step] = e.astype(BF)

    def all_of(k, phase, ref):
        return remote(ref, ref, as_sem.at[k, phase], ar_sem.at[k, phase], groups[NEAR][0])

    def split(k):
        for i, p in enumerate(groups[ORDERS[k][0]]):
            remote(
                grads.at[k, pl.ds(place(p), chunk)], got.at[k, 0, i], as_sem.at[k, 0], ar_sem.at[k, 0], p
            ).start()

    def add(k, phase):
        all_of(k, phase, got.at[k, phase]).wait_recv()
        own = grads[k, pl.ds(place(me), chunk), :] if phase == 0 else part[k, phase - 1]
        return tree([own] + [got[k, phase, FAR_FIRST.index(d)] for d in range(1, GROUP)])

    def share(k, phase):
        part[k, phase] = add(k, phase)
        for i, p in enumerate(groups[ORDERS[k][phase + 1]]):
            remote(
                part.at[k, phase], got.at[k, phase + 1, i],
                as_sem.at[k, phase + 1], ar_sem.at[k, phase + 1], p,
            ).start()

    def gather(k):
        here = full.at[k, pl.ds(place(me), chunk)]
        full[k, pl.ds(place(me), chunk), :] = add(k, 2)
        for p in groups[NEAR]:
            remote(here, here, as_sem.at[k, 3], ar_sem.at[k, 3], p).start()

    def finish(k):
        rest = full.at[k, pl.ds(0, width - chunk)]
        all_of(k, 3, rest).wait_recv()
        grads_o[k] = full[k]
        for phase in range(3):
            all_of(k, phase, got.at[k, phase]).wait_send()
        all_of(k, 3, rest).wait_send()

    grads[0] = dot(err_bt[...], agg2[...])
    split(0)
    cot = dot(w2[...], err_bt[...]).astype(BF)
    near = ((err_t[...] + dot(cot, bonds[...])) * slope_t[...]).astype(BF)
    far = (dot(cot, halo[...]) * slope_far_t[...]).astype(BF)
    grads[1] = dot(near, agg1[...]) + dot(far, in_buf[1])
    split(1)
    for phase in range(2):
        share(0, phase)
        share(1, phase)
    gather(0)
    gather(1)
    for c in first + second:
        c.wait_send()
    finish(0)
    finish(1)


def write_out(pred_i, grads_i, pred_o, g1_o, g2_o):
    pred_o[...] = pred_i[...]
    g2_o[...] = grads_i[0].T
    g1_o[...] = grads_i[1].T


def make_local(n):
    def local(features, targets, first_weight, second_weight, local_bonds, halo_bonds, tile_mask, send_rows):
        rows, width = features.shape
        hw = ROUNDS * send_rows.shape[1]
        chunk = width // GROUP
        hbm = pl.BlockSpec(memory_space=pltpu.HBM)
        vmem = pl.BlockSpec(memory_space=pltpu.VMEM)
        args = (features, targets, first_weight, second_weight, local_bonds, halo_bonds, tile_mask, send_rows)
        pred, grads = pl.pallas_call(
            functools.partial(body, rows * n),
            out_shape=(
                pltpu.VMEM((rows, width), BF),
                pltpu.VMEM((2, width, width), F32),
            ),
            in_specs=[hbm] * 8,
            out_specs=(vmem, vmem),
            scratch_shapes=[pltpu.VMEM(a.shape, a.dtype) for a in args]
            + [
                pltpu.VMEM((tile_mask.shape[0], rows), F32),
                pltpu.VMEM((hw, rows), BF),
                pltpu.VMEM((rows, 2 * width), BF),
                pltpu.VMEM((hw, hw), BF),
                pltpu.VMEM((hw, width), F32),
                pltpu.VMEM((rows, width), F32),
                pltpu.VMEM((rows, width), BF),
                pltpu.VMEM((rows, width), BF),
                pltpu.VMEM((hw, width), BF),
                pltpu.VMEM((rows, width), BF),
                pltpu.VMEM((width, rows), F32),
                pltpu.VMEM((width, rows), BF),
                pltpu.VMEM((width, rows), F32),
                pltpu.VMEM((width, hw), F32),
                pltpu.VMEM((2, hw, width), BF),
                pltpu.VMEM((2, hw, width), BF),
                pltpu.VMEM((2, width, width), F32),
                pltpu.VMEM((2, 3, GROUP - 1, chunk, width), F32),
                pltpu.VMEM((2, 2, chunk, width), F32),
                pltpu.VMEM((2, width, width), F32),
                pltpu.SemaphoreType.DMA((8,)),
                pltpu.SemaphoreType.DMA((2, ROUNDS)),
                pltpu.SemaphoreType.DMA((2, ROUNDS)),
                pltpu.SemaphoreType.DMA((2, 4)),
                pltpu.SemaphoreType.DMA((2, 4)),
            ],
            compiler_params=pltpu.CompilerParams(
                collective_id=0, has_side_effects=True,
            ),
            name="step",
        )(*args)
        return pl.pallas_call(
            write_out,
            out_shape=(
                jax.ShapeDtypeStruct((rows, width), BF),
                jax.ShapeDtypeStruct((width, width), F32),
                jax.ShapeDtypeStruct((width, width), F32),
            ),
            in_specs=[vmem] * 2,
            out_specs=(vmem, vmem, vmem),
            compiler_params=pltpu.CompilerParams(vmem_limit_bytes=4 << 20),
            name="write_out",
        )(pred, grads)

    return local


def solution(mesh):
    split = P("dom", None)
    return jax.shard_map(
        make_local(mesh.shape["dom"]),
        mesh=mesh,
        in_specs=(split, split, P(), P(), split, split, split, split),
        out_specs=(split, P(), P()),
        check_vma=False,
    )
```

```python
import functools
import math

import jax
import jax.numpy as jnp
from jax import lax
from jax.experimental import pallas as pl
from jax.experimental.pallas import tpu as pltpu
from jax.sharding import PartitionSpec as P

MESH = pl.DeviceIdType.MESH
ROUNDS = 4
BF = jnp.bfloat16
F32 = jnp.float32
NEAR, YAXIS, ZAXIS = (0, 7, 8), (4, 5, 6), (1, 2, 3)
ORDERS = ((NEAR, ZAXIS, YAXIS), (NEAR, YAXIS, ZAXIS))
GROUP = 8
FAR_FIRST = (4, 5, 3, 7, 6, 2, 1)


def dot(a, b):
    return jnp.dot(a, b, preferred_element_type=F32)


def tree(values):
    while len(values) > 1:
        values = [values[i] + values[i + 1] for i in range(0, len(values), 2)]
    return values[0]


def body(
    nodes,
    feat_h, targ_h, w1_h, w2_h, bonds_h, halo_h, mask_h, send_h,
    pred, grads_o,
    feat, targ, w1, w2, bonds, halo, mask, send,
    spread, hot, halves, halo_sent, sent, inner, agg1, hid, hid_far, agg2, err_t, err_bt, slope_t, slope_far_t,
    out_buf, in_buf, grads, got, part, full,
    load_sem, hs_sem, hr_sem, as_sem, ar_sem,
):
    rows, width = feat.shape
    step = 384
    blocks = [pl.ds(i, step) for i in range(0, rows, step)]
    hw = send.shape[1]
    chunk = width // GROUP

    def load(i, a, b):
        copy = pltpu.make_async_copy(a, b, load_sem.at[i])
        copy.start()
        return copy

    c_send = load(1, send_h, send)
    c_feat = load(0, feat_h, feat)
    c_mask = load(2, mask_h, mask)
    c_bonds = load(3, bonds_h, bonds)
    c_halo = load(4, halo_h, halo)
    c_w1 = load(5, w1_h, w1)
    c_w2 = load(6, w2_h, w2)
    c_targ = load(7, targ_h, targ)

    me = lax.axis_index("dom")
    delta = [(1 << b) * (1 - 2 * lax.rem(lax.div(me, 1 << b), 2)) for b in range(9)]

    def peers(bits):
        return [
            me + sum(delta[b] for j, b in enumerate(bits) if (d >> j) & 1) for d in FAR_FIRST
        ]

    groups = {bits: peers(bits) for bits in (NEAR, YAXIS, ZAXIS)}

    def place(device):
        return pl.multiple_of((lax.rem(device, 2) + 2 * lax.div(device, 128)) * chunk, chunk)

    barrier = pltpu.get_barrier_semaphore()
    for bits in (ZAXIS, YAXIS, NEAR):
        for p in groups[bits]:
            pl.semaphore_signal(barrier, inc=1, device_id=(p,), device_id_type=MESH)

    def remote(src, dst, ss, rs, p):
        return pltpu.make_async_remote_copy(
            src_ref=src, dst_ref=dst, send_sem=ss, recv_sem=rs, device_id=(p,), device_id_type=MESH
        )

    def exchange(k):
        copies = []
        for r in reversed(range(ROUNDS)):
            c = remote(
                out_buf.at[k, pl.ds(r * hw, hw)], in_buf.at[k, pl.ds(r * hw, hw)],
                hs_sem.at[k, r], hr_sem.at[k, r], me + delta[r],
            )
            c.start()
            copies.append(c)
        return copies

    c_send.wait()
    for r in range(ROUNDS):
        wanted = jnp.broadcast_to(send[r : r + 1, :].astype(F32), (hw, hw)).T.astype(jnp.int32)
        lane = lax.broadcasted_iota(jnp.int32, (hw, hw), 1)
        for c in range(0, rows, hw):
            hot[r * hw : (r + 1) * hw, c : c + hw] = (wanted == lane + c).astype(F32).astype(BF)
    c_feat.wait()
    out_buf[0] = dot(hot[...], feat[...]).astype(BF)

    c_mask.wait()
    tiles = mask.shape[0]
    tile = rows // tiles
    col = lax.broadcasted_iota(jnp.int32, (tiles, rows), 1)
    total = jnp.zeros((tiles, rows), F32)
    for t in range(tiles):
        inside = (col >= t * tile) & (col < (t + 1) * tile)
        total = total + jnp.where(inside, mask[:, t : t + 1].astype(F32), 0.0)
    spread[...] = total
    c_bonds.wait()
    for t in range(tiles):
        here = pl.ds(t * tile, tile)
        bonds[here, :] = bonds[here, :] * spread[t : t + 1, :].astype(BF)
    pl.semaphore_wait(barrier, 3 * (GROUP - 1))
    first = exchange(0)

    for b in blocks:
        v = dot(bonds[b, :], feat[...])
        inner[b, :] = v
        high = v.astype(BF)
        halves[b, :width] = high
        halves[b, width:] = (v - high.astype(F32)).astype(BF)
    c_halo.wait()
    halo_sent[...] = dot(hot[...], halo[...]).astype(BF)
    both = dot(hot[...], halves[...])
    sent[...] = both[:, :width] + both[:, width:]
    c_w1.wait()
    last = (ROUNDS - 1) * hw
    for c in first[1:]:
        c.wait_recv()
    sent[...] += dot(halo_sent[:, :last], in_buf[0, :last, :])
    first[0].wait_recv()

    out_buf[1] = (sent[...] + dot(halo_sent[:, last:], in_buf[0, last:, :])).astype(BF)
    second = exchange(1)

    def activate(a, x):
        u = dot(a, w1[...])
        s = jax.nn.sigmoid(u)
        return (x.astype(F32) + u * s).astype(BF), s * (1.0 + u * (1.0 - s))

    for i in range(0, rows, step):
        b = pl.ds(i, step)
        a = (inner[b, :] + dot(halo[b, :], in_buf[0])).astype(BF)
        agg1[b, :] = a
        hid[b, :], slope = activate(a, feat[b, :])
        slope_t[:, i : i + step] = slope.T
    c_w2.wait()
    c_targ.wait()
    for c in second[1:]:
        c.wait_recv()
    hid_far[:last, :], slope = activate(in_buf[1, :last, :], in_buf[0, :last, :])
    slope_far_t[:, :last] = slope.T
    for b in blocks:
        inner[b, :] = dot(bonds[b, :], hid[...]) + dot(halo[b, :last], hid_far[:last, :])
    second[0].wait_recv()
    hid_far[last:, :], slope = activate(in_buf[1, last:, :], in_buf[0, last:, :])
    slope_far_t[:, last:] = slope.T
    scale = 1.0 / math.sqrt(nodes)
    for i in range(0, rows, step):
        b = pl.ds(i, step)
        a = (inner[b, :] + dot(halo[b, last:], hid_far[last:, :])).astype(BF)
        agg2[b, :] = a
        o = hid[b, :].astype(F32) + dot(a, w2[...])
        pred[b, :] = o.astype(BF)
        e = ((o - targ[b, :].astype(F32)) * scale).T
        err_t[:, i : i + step] = e
        err_bt[:, i : i + step] = e.astype(BF)

    def all_of(k, phase, ref):
        return remote(ref, ref, as_sem.at[k, phase], ar_sem.at[k, phase], groups[NEAR][0])

    def split(k):
        for i, p in enumerate(groups[ORDERS[k][0]]):
            remote(
                grads.at[k, pl.ds(place(p), chunk)], got.at[k, 0, i], as_sem.at[k, 0], ar_sem.at[k, 0], p
            ).start()

    def add(k, phase):
        all_of(k, phase, got.at[k, phase]).wait_recv()
        own = grads[k, pl.ds(place(me), chunk), :] if phase == 0 else part[k, phase - 1]
        return tree([own] + [got[k, phase, FAR_FIRST.index(d)] for d in range(1, GROUP)])

    def share(k, phase):
        part[k, phase] = add(k, phase)
        for i, p in enumerate(groups[ORDERS[k][phase + 1]]):
            remote(
                part.at[k, phase], got.at[k, phase + 1, i],
                as_sem.at[k, phase + 1], ar_sem.at[k, phase + 1], p,
            ).start()

    def gather(k):
        here = full.at[k, pl.ds(place(me), chunk)]
        full[k, pl.ds(place(me), chunk), :] = add(k, 2)
        for p in groups[NEAR]:
            remote(here, here, as_sem.at[k, 3], ar_sem.at[k, 3], p).start()

    def finish(k):
        rest = full.at[k, pl.ds(0, width - chunk)]
        all_of(k, 3, rest).wait_recv()
        grads_o[k] = full[k]
        for phase in range(3):
            all_of(k, phase, got.at[k, phase]).wait_send()
        all_of(k, 3, rest).wait_send()

    grads[0] = dot(err_bt[...], agg2[...])
    split(0)
    cot = dot(w2[...], err_bt[...]).astype(BF)
    near = ((err_t[...] + dot(cot, bonds[...])) * slope_t[...]).astype(BF)
    far = (dot(cot, halo[...]) * slope_far_t[...]).astype(BF)
    grads[1] = dot(near, agg1[...]) + dot(far, in_buf[1])
    split(1)
    for phase in range(2):
        share(0, phase)
        share(1, phase)
    gather(0)
    gather(1)
    for c in first + second:
        c.wait_send()
    finish(0)
    finish(1)


def write_out(pred_i, grads_i, pred_o, g1_o, g2_o):
    pred_o[...] = pred_i[...]
    g2_o[...] = grads_i[0].T
    g1_o[...] = grads_i[1].T


def make_local(n):
    def local(features, targets, first_weight, second_weight, local_bonds, halo_bonds, tile_mask, send_rows):
        rows, width = features.shape
        hw = ROUNDS * send_rows.shape[1]
        chunk = width // GROUP
        hbm = pl.BlockSpec(memory_space=pltpu.HBM)
        vmem = pl.BlockSpec(memory_space=pltpu.VMEM)
        args = (features, targets, first_weight, second_weight, local_bonds, halo_bonds, tile_mask, send_rows)
        pred, grads = pl.pallas_call(
            functools.partial(body, rows * n),
            out_shape=(
                pltpu.VMEM((rows, width), BF),
                pltpu.VMEM((2, width, width), F32),
            ),
            in_specs=[hbm] * 8,
            out_specs=(vmem, vmem),
            scratch_shapes=[pltpu.VMEM(a.shape, a.dtype) for a in args]
            + [
                pltpu.VMEM((tile_mask.shape[0], rows), F32),
                pltpu.VMEM((hw, rows), BF),
                pltpu.VMEM((rows, 2 * width), BF),
                pltpu.VMEM((hw, hw), BF),
                pltpu.VMEM((hw, width), F32),
                pltpu.VMEM((rows, width), F32),
                pltpu.VMEM((rows, width), BF),
                pltpu.VMEM((rows, width), BF),
                pltpu.VMEM((hw, width), BF),
                pltpu.VMEM((rows, width), BF),
                pltpu.VMEM((width, rows), F32),
                pltpu.VMEM((width, rows), BF),
                pltpu.VMEM((width, rows), F32),
                pltpu.VMEM((width, hw), F32),
                pltpu.VMEM((2, hw, width), BF),
                pltpu.VMEM((2, hw, width), BF),
                pltpu.VMEM((2, width, width), F32),
                pltpu.VMEM((2, 3, GROUP - 1, chunk, width), F32),
                pltpu.VMEM((2, 2, chunk, width), F32),
                pltpu.VMEM((2, width, width), F32),
                pltpu.SemaphoreType.DMA((8,)),
                pltpu.SemaphoreType.DMA((2, ROUNDS)),
                pltpu.SemaphoreType.DMA((2, ROUNDS)),
                pltpu.SemaphoreType.DMA((2, 4)),
                pltpu.SemaphoreType.DMA((2, 4)),
            ],
            compiler_params=pltpu.CompilerParams(
                collective_id=0, has_side_effects=True,
            ),
            name="step",
        )(*args)
        return pl.pallas_call(
            write_out,
            out_shape=(
                jax.ShapeDtypeStruct((rows, width), BF),
                jax.ShapeDtypeStruct((width, width), F32),
                jax.ShapeDtypeStruct((width, width), F32),
            ),
            in_specs=[vmem] * 2,
            out_specs=(vmem, vmem, vmem),
            compiler_params=pltpu.CompilerParams(vmem_limit_bytes=4 << 20),
            name="write_out",
        )(pred, grads)

    return local


def solution(mesh):
    split = P("dom", None)
    return jax.shard_map(
        make_local(mesh.shape["dom"]),
        mesh=mesh,
        in_specs=(split, split, P(), P(), split, split, split, split),
        out_specs=(split, P(), P()),
        check_vma=False,
    )
```
